256 devices in a mesh: mem: 32 (over x, y, core), row: 8 (over z).
Axes of the slice: x: 4, y: 4, z: 8, core: 2. Of those that a mesh axis runs over, the one named last changes fastest.
Arguments:
- predicted_surpass_tally: int32 [32, 1024, 4096], P('mem', 'row'), may hold values from 0 to 1, as said below
- observed_surpass_tally: int32 [1024, 4096], P('row'), may hold values from 0 to 1, as said below
Outputs:
- energy_maps: float32 [1, 8, 1024, 4096], P(None, None, 'row', 'mem')
- skill: float32 [32, 1, 8], P('mem')
The draws below stay inside these ranges and needn't reach their ends.
Inputs may be any that keep to these rules, and one draw needn't show every extreme that they name: `predicted_surpass_tally`: A cell that exceeds a threshold exceeds every lower one, so the mask of threshold t is the class being greater than t. `observed_surpass_tally`: coded as predicted_surpass_tally.
All inputs are finite; a program needn't handle non-finite values.
Results may differ from the reference program's by a relative error of at most 0.0003.
Values sent between devices are 32-bit elements; how exact they have to be, the bound alone decides.
A program may use at most 64 MiB of HBM per device.

```python
import jax
import jax.numpy as jnp
from jax import lax

NCOLS = 4096
NT = 1
LEVELS = 7
MEMBERS = 32
NROWS = 1024


def analysis_classes(key):
    uniform_int = jax.random.randint(jax.random.fold_in(key, 11), (NROWS, NCOLS), 0, 4096)
    row_index = lax.broadcasted_iota(jnp.int32, (NROWS, NCOLS), 0)
    classes = jnp.zeros((NROWS, NCOLS), jnp.int32)
    for thresh in range(NT):
        bound = 1200 // (thresh + 1) * (NROWS + 2 * row_index) // NROWS
        classes = classes + (uniform_int < bound).astype(jnp.int32)
    return classes


def draw_observed_surpass_tally(key, part):
    return analysis_classes(key)


def draw_predicted_surpass_tally(key, part):
    analysis = analysis_classes(key)
    shape = (MEMBERS, NROWS, NCOLS)
    row_index = lax.broadcasted_iota(jnp.int32, shape, 1)
    flip_draw = jax.random.randint(jax.random.fold_in(key, 23), shape, 0, 4096)
    fresh = jax.random.randint(jax.random.fold_in(key, 29), shape, 0, NT + 1)
    flipped = flip_draw < 300 * (NROWS + 2 * row_index) // NROWS
    return jnp.where(flipped, fresh, analysis[None, :, :]).astype(jnp.int32)


def setup_inputs(seed: int = 0) -> dict:
    key_of = jax.random.split(jax.random.key(seed), 3)
    predicted_surpass_tally = draw_predicted_surpass_tally(jax.random.fold_in(key_of[2], 71), 0)
    observed_surpass_tally = draw_observed_surpass_tally(jax.random.fold_in(key_of[2], 71), 0)
    return {"predicted_surpass_tally": predicted_surpass_tally, "observed_surpass_tally": observed_surpass_tally}


KERNEL = (1.0 / 16.0, 4.0 / 16.0, 6.0 / 16.0, 4.0 / 16.0, 1.0 / 16.0)


def column_pass(field, spacing):
    breadth = field.shape[1]
    padded = jnp.pad(field, ((0, 0), (2 * spacing, 2 * spacing)))
    result = KERNEL[0] * padded[:, 0:breadth]
    for index in range(1, 5):
        result = result + KERNEL[index] * padded[:, index * spacing:index * spacing + breadth]
    return result


def row_pass(padded, spacing, height):
    result = KERNEL[0] * padded[0:height]
    for index in range(1, 5):
        result = result + KERNEL[index] * padded[index * spacing:index * spacing + height]
    return result


def smooth_field(field, spacing):
    across = column_pass(field, spacing)
    padded = jnp.pad(across, ((2 * spacing, 2 * spacing), (0, 0)))
    return row_pass(padded, spacing, field.shape[0])


def decompose(field):
    pieces = []
    current = field
    for level in range(1, LEVELS + 1):
        smoother = smooth_field(current, 2 ** (level - 1))
        pieces.append(current - smoother)
        current = smoother
    pieces.append(current)
    return pieces


def reference(predicted_surpass_tally, observed_surpass_tally):
    height, breadth = observed_surpass_tally.shape
    cells = float(height * breadth)
    observed = jnp.stack([(observed_surpass_tally > thresh).astype(jnp.float32) for thresh in range(NT)])
    base_rate = jnp.sum(observed, axis=(1, 2)) / cells
    weights = [4.0 ** min(level + 1, LEVELS) for level in range(LEVELS + 1)]

    def realization_increment(level_power_amount, realization_surpass_tally):
        weighted = []
        cumulative_accumulations = []
        for thresh in range(NT):
            error_field = (realization_surpass_tally > thresh).astype(jnp.float32) - observed[thresh]
            pieces = decompose(error_field)
            for level in range(LEVELS + 1):
                squared = pieces[level] * pieces[level]
                weighted.append(squared * weights[level])
                cumulative_accumulations.append(jnp.sum(squared))
        level_power_amount = level_power_amount + jnp.stack(weighted).reshape(NT, LEVELS + 1, height, breadth)
        return level_power_amount, jnp.stack(cumulative_accumulations).reshape(NT, LEVELS + 1)

    start_position = jnp.zeros((NT, LEVELS + 1, height, breadth), jnp.float32)
    level_power_amount, cumulative_accumulations = lax.scan(realization_increment, start_position, predicted_surpass_tally)
    mean_error = cumulative_accumulations / cells
    spread = 2.0 * base_rate * (1.0 - base_rate)
    skill = 1.0 - mean_error * (LEVELS + 1) / spread[None, :, None]
    return level_power_amount / MEMBERS, skill
```

```python
import functools

import jax
import jax.numpy as jnp
from jax import lax
from jax.experimental import pallas as pl
from jax.experimental.pallas import tpu as pltpu
from jax.sharding import PartitionSpec as P

MESH = pl.DeviceIdType.MESH
F32, BF16 = jnp.float32, jnp.bfloat16

LEVELS = 7
H = 128
W = 4096
TILE = 256
TILES = W // TILE
SIDE = 4
ROWS = 8
MEMBERS = 32
TAPS = (1.0 / 16.0, 4.0 / 16.0, 6.0 / 16.0, 4.0 / 16.0, 1.0 / 16.0)
WEIGHTS = [4.0 ** min(k + 1, LEVELS) for k in range(LEVELS + 1)]
PAD = 128

SLOT_ROW = (128, 384, 0, 512)
HALO = (
    (0, 1, 112, 16),
    (1, -1, 0, 16),
    (0, 1, 64, 48),
    (1, -1, 16, 48),
    (0, 1, 0, 64),
    (1, -1, 64, 64),
    (2, 2, 32, 96),
    (3, -2, 0, 96),
    (2, 2, 0, 32),
    (3, -2, 96, 32),
)
PIECES = [[(k, 0), (k, 32), (k, 64), (k, 96)] for k in range(6)]
PIECES += [[(6, 32), (6, 64), (7, 32), (7, 64)], [(6, 0), (6, 96), (7, 0), (7, 96)]]
BLOCK = 32


def kernel(
    e_ref, obs_ref, out_ref, skill_ref,
    halo, ext, ub, sb, part, pair, ring1, ring2, xr, rm, rm7, xe, xi, ci, ce, obuf, acc, peers,
    osem, zsend, zrecv, psend, precv, ksend, krecv,
):
    mem, row = lax.axis_index("mem"), lax.axis_index("row")
    c, y, x = lax.rem(mem, 2), lax.rem(mem // 2, SIDE), mem // (2 * SIDE)

    def at(xx, yy, cc):
        return (xx * SIDE + yy) * 2 + cc

    def along_z(step):
        return (mem, lax.rem(row + step + ROWS, ROWS))

    def along(axis, step):
        if axis == "y":
            return (at(x, lax.rem(y + step + SIDE, SIDE), c), row)
        return (at(lax.rem(x + step + SIDE, SIDE), y, c), row)

    sibling = (at(x, y, 1 - c), row)

    barrier = pltpu.get_barrier_semaphore()
    partners = [along_z(d) for d in range(1, ROWS)] + [sibling]
    partners += [along(axis, d) for axis in "xy" for d in (1, -1)]
    for partner in partners:
        pl.semaphore_signal(barrier, inc=1, device_id=partner, device_id_type=MESH)
    pl.semaphore_wait(barrier, len(partners))

    sends = []

    def remote(src, dst, send, recv, target):
        copy = pltpu.make_async_remote_copy(
            src_ref=src, dst_ref=dst, send_sem=send, recv_sem=recv, device_id=target, device_id_type=MESH
        )
        copy.start()
        sends.append(copy)
        return copy

    halos = []
    for n, (slot, step, first, rows) in enumerate(HALO):
        span = pl.ds(first, rows)
        halos.append(remote(e_ref.at[span, :], halo.at[slot, span, :], zsend.at[n], zrecv.at[n], along_z(step)))

    def take(n):
        slot, _, first, rows = HALO[n]
        halos[n].wait_recv()

        @pl.loop(0, W // 512)
        def _(i):
            lanes = pl.ds(pl.multiple_of(i * 512, 512), 512)
            ext[SLOT_ROW[slot] + first : SLOT_ROW[slot] + first + rows, lanes] = halo[
                slot, first : first + rows, lanes
            ].astype(BF16)

    @pl.loop(0, W // 512)
    def _(i):
        lanes = pl.ds(pl.multiple_of(i * 512, 512), 512)
        ext[256:384, lanes] = e_ref[:, lanes].astype(BF16)
        for first, rows in ((0, 32), (128, 128), (384, 128), (608, 32)):
            ext[first : first + rows, lanes] = jnp.zeros((rows, 512), BF16)

    acc[...] = jnp.zeros_like(acc)

    def taps(load, spacing):
        a, b, m, d, e = (load((q - 2) * spacing) for q in range(5))
        return TAPS[0] * (a + e) + TAPS[1] * (b + d) + TAPS[2] * m

    def split(value):
        high = value.astype(BF16)
        return high, (value - high.astype(F32)).astype(BF16)

    for side in range(2):
        xr[side, 0:PAD, :] = jnp.zeros((PAD, 128), F32)
        xr[side, PAD + 640 : 2 * PAD + 640, :] = jnp.zeros((PAD, 128), F32)
    for lane_block in range(5):
        index = lax.broadcasted_iota(jnp.int32, (640, 128), 0)
        domain = index + (row * H - 256)
        inside = (domain >= 0) & (domain < ROWS * H)
        lane = lax.broadcasted_iota(jnp.int32, (640, 128), 1) + lane_block * 128
        xr[0, PAD : PAD + 640, :] = jnp.where(inside & (index == lane), 1.0, 0.0)
        for level in range(1, LEVELS + 1):
            src, dst = (level + 1) % 2, level % 2
            new = taps(lambda o: xr[src, PAD + o : PAD + o + 640, :], 2 ** (level - 1))
            xr[dst, PAD : PAD + 640, :] = jnp.where(inside, new, 0.0)
            high, low = split(xr[dst, PAD + 256 : PAD + 384, :])
            if level == LEVELS:
                rm7[0:H, lane_block * 128 : lane_block * 128 + 128] = high
                rm7[H : 2 * H, lane_block * 128 : lane_block * 128 + 128] = low
            elif 1 <= lane_block <= 3:
                rm[level - 1, 0:H, lane_block * 128 - 128 : lane_block * 128] = high
                rm[level - 1, H : 2 * H, lane_block * 128 - 128 : lane_block * 128] = low

    for side in range(2):
        for start in (0, PAD + 768):
            xi[side, start : start + PAD, :] = jnp.zeros((PAD, TILE), F32)
        for start in (0, PAD + 512):
            xe[side, start : start + PAD, :] = jnp.zeros((PAD, 512), F32)
    xi[0, PAD : PAD + 768, :] = jnp.where(
        lax.broadcasted_iota(jnp.int32, (768, TILE), 0) - 256 == lax.broadcasted_iota(jnp.int32, (768, TILE), 1),
        1.0, 0.0,
    )
    xe[0, PAD : PAD + 512, :] = jnp.where(
        lax.broadcasted_iota(jnp.int32, (512, 512), 0) == lax.broadcasted_iota(jnp.int32, (512, 512), 1), 1.0, 0.0
    )

    def column_operators(level):
        src, dst = (level + 1) % 2, level % 2
        spacing = 2 ** (level - 1)

        @pl.loop(0, TILE // 128)
        def _(i):
            lanes = pl.ds(pl.multiple_of(i * 128, 128), 128)
            new = taps(lambda o: xi[src, PAD + o : PAD + o + 768, lanes], spacing)
            xi[dst, PAD : PAD + 768, lanes] = new
            ci[0, :, lanes], ci[1, :, lanes] = split(new)

        @pl.loop(0, 512 // 128)
        def _(i):
            lanes = pl.ds(pl.multiple_of(i * 128, 128), 128)
            new = taps(lambda o: xe[src, PAD + o : PAD + o + 512, lanes], spacing)
            xe[dst, PAD : PAD + 512, lanes] = new
            ce[0, :, lanes], ce[1, :, lanes] = split(new)

    def level_pass(level, spans):
        reach = 256 if level == LEVELS else 128
        height = sum(rows for _, rows in spans)
        ops = rm7 if level == LEVELS else rm.at[level - 1]
        depth = slice(0, 640) if level == LEVELS else slice(128, 512)

        def pick(ref, offset):
            return [ref[offset + first : offset + first + rows, :] for first, rows in spans]

        @pl.loop(0, TILES)
        def _(t):
            lanes = pl.ds(pl.multiple_of(t * TILE, TILE), TILE)
            left = jnp.concatenate(pick(ops, 0) + pick(ops, H), axis=0)
            both = jnp.dot(left, ext[depth, lanes], preferred_element_type=F32)
            high, low = split(both[:height] + both[height:])
            done = 0
            for first, rows in spans:
                ub[t, first : first + rows, :] = high[done : done + rows]
                ub[t, H + first : H + first + rows, :] = low[done : done + rows]
                done += rows

        def finish(t, both, cross):
            smooth = both[:height] + both[height:] + cross
            lanes = pl.ds(pl.multiple_of(t * TILE, TILE), TILE) if not isinstance(t, int) else pl.ds(t * TILE, TILE)
            done = 0
            for first, rows in spans:
                now = smooth[done : done + rows]
                before = e_ref[first : first + rows, lanes] if level == 1 else sb[t, first : first + rows, :]
                store(level - 1, t, first, rows, before - now)
                if level == LEVELS:
                    store(LEVELS, t, first, rows, now)
                else:
                    sb[t, first : first + rows, :] = now
                done += rows

        def store(k, t, first, rows, component):
            energy = component * component * (WEIGHTS[k] / MEMBERS)
            for core in range(2):
                part[k, core, t // SIDE, t % SIDE, first : first + rows, :] = energy[:, core * 128 : core * 128 + 128]
            folded = energy[:, 0:128] + energy[:, 128:256]
            acc[k] += jnp.sum(folded.reshape(rows // 8, 8, 128), axis=0)

        def lhs(tiles):
            return jnp.concatenate(
                [
                    jnp.concatenate(
                        [ub[t, offset + first : offset + first + rows, lanes] for t, lanes in tiles], axis=1
                    )
                    for offset in (0, H)
                    for first, rows in spans
                ],
                axis=0,
            )

        near_left, whole, near_right = slice(256 - reach, 256), slice(0, 256), slice(0, reach)

        @pl.loop(1, TILES - 1)
        def _(t):
            left = lhs([(t - 1, near_left), (t, whole), (t + 1, near_right)])
            depth = slice(256 - reach, 512 + reach)
            both = jnp.dot(left, ci[0, depth, :], preferred_element_type=F32)
            cross = jnp.dot(left[:height], ci[1, depth, :], preferred_element_type=F32)
            finish(t, both, cross)

        for t, tiles, out, depth in (
            (0, [(0, whole), (1, near_right)], slice(0, 256), slice(0, 256 + reach)),
            (TILES - 1, [(TILES - 2, near_left), (TILES - 1, whole)], slice(256, 512), slice(256 - reach, 512)),
        ):
            left = lhs(tiles)
            dims = (((1,), (1,)), ((), ()))
            both = lax.dot_general(left, ce[0, out, depth], dims, preferred_element_type=F32)
            cross = lax.dot_general(left[:height], ce[1, out, depth], dims, preferred_element_type=F32)
            finish(t, both, cross)

    flights = {}

    def block_of(p, i, axis, pos, stage):
        k, first = PIECES[p][i]
        rows = pl.ds(first, BLOCK)
        if stage == 1:
            if axis == "y":
                return part.at[k, c, :, pos, rows, :]
            return part.at[k, c, pos, :, rows, :]
        if axis == "y":
            return part.at[k, c, x, pos, rows, :]
        return part.at[k, c, pos, y, rows, :]

    def axis_of(half, stage):
        return "yx"[(half + stage - 1) % 2]

    def spot(axis, step):
        return lax.rem((y if axis == "y" else x) + step + SIDE, SIDE)

    def pair_start(p):
        for i, (k, first) in enumerate(PIECES[p]):
            rows = pl.ds(first, BLOCK)
            flights[p, 0, i] = remote(
                part.at[k, 1 - c, :, :, rows, :], pair.at[k, :, :, rows, :], psend.at[p, i], precv.at[p, i], sibling
            )

    def ring_copy(p, stage, half, n, i, pos, step):
        axis = axis_of(half, stage)
        landing = (ring1 if stage == 1 else ring2).at[p, half, n]
        sem = 4 + (stage - 1) * 12 + half * 6 + n
        flights[p, stage, half, n] = remote(
            block_of(p, i, axis, spot(axis, pos), stage), landing, psend.at[p, sem], precv.at[p, sem], along(axis, step)
        )

    def ring_start(p, stage):
        for half in range(2):
            i0, i1 = 2 * half, 2 * half + 1
            ring_copy(p, stage, half, 0, i0, 2, 1)
            ring_copy(p, stage, half, 1, i1, 2, -1)
            ring_copy(p, stage, half, 2, i1, 1, 1)
            ring_copy(p, stage, half, 3, i0, -1, -1)

    def ring_add(p, stage, half, n, i, pos):
        axis = axis_of(half, stage)
        flights[p, stage, half, n].wait_recv()
        block = block_of(p, i, axis, spot(axis, pos), stage)
        block[...] = block[...] + (ring1 if stage == 1 else ring2)[p, half, n]

    def ring_middle(p, stage):
        for half in range(2):
            i0, i1 = 2 * half, 2 * half + 1
            ring_add(p, stage, half, 0, i0, 1)
            ring_copy(p, stage, half, 4, i0, 1, 1)
            ring_add(p, stage, half, 1, i1, -1)
            ring_copy(p, stage, half, 5, i1, -1, -1)

    def ring_end(p, stage):
        for half in range(2):
            i0, i1 = 2 * half, 2 * half + 1
            ring_add(p, stage, half, 3, i0, 0)
            ring_add(p, stage, half, 2, i1, 0)
            ring_add(p, stage, half, 4, i0, 0)
            ring_add(p, stage, half, 5, i1, 0)

    def advance(p, step):
        if step == 0:
            pair_start(p)
        elif step == 1:
            for i, (k, first) in enumerate(PIECES[p]):
                flights[p, 0, i].wait_recv()

                @pl.loop(0, SIDE)
                def _(j):
                    rows = pl.ds(first, BLOCK)
                    part[k, c, j, :, rows, :] = part[k, c, j, :, rows, :] + pair[k, j, :, rows, :]

            ring_start(p, 1)
        elif step == 2:
            ring_middle(p, 1)
        elif step == 3:
            ring_end(p, 1)
            ring_start(p, 2)
        elif step == 4:
            ring_middle(p, 2)
        elif step == 5:
            ring_end(p, 2)
            for k, first in PIECES[p]:
                out_ref[k, first : first + BLOCK, :] = part[k, c, x, y, pl.ds(first, BLOCK), :]

    position = {}

    def tick(limit):
        for p in sorted(position):
            if p <= limit and position[p] < 5:
                position[p] += 1
                advance(p, position[p])

    def begin(p):
        position[p] = 0
        advance(p, 0)

    everything = [(0, H)]
    for level in range(1, LEVELS):
        column_operators(level)
        if level == 1:
            take(0), take(1)
        if level == 4:
            take(2), take(3)
        if level == 6:
            take(4), take(5)
        level_pass(level, everything)
        tick(level - 2)
        begin(level - 1)

    @pl.loop(0, W // 512)
    def _(i):
        copy = pltpu.make_async_copy(obs_ref.at[:, pl.ds(pl.multiple_of(i * 512, 512), 512)], obuf, osem)
        copy.start()
        copy.wait()
        seen = jnp.where(obuf[...] > 0, 1.0, 0.0)
        acc[LEVELS + 1] += jnp.sum(jnp.sum(seen.reshape(16, 8, 4, 128), axis=0), axis=1)

    column_operators(LEVELS)
    while any(position[p] < 5 for p in range(6)):
        tick(5)

    take(6), take(7)
    level_pass(LEVELS, [(32, 64)])
    begin(6)
    tick(6)
    tick(6)
    take(8), take(9)
    level_pass(LEVELS, [(0, 32), (96, 32)])
    begin(7)

    tallies = [
        remote(acc, peers.at[d - 1], ksend.at[d - 1], krecv.at[d - 1], along_z(d)) for d in range(1, ROWS)
    ]
    while any(position[p] < 5 for p in position):
        tick(7)

    for copy in tallies:
        copy.wait_recv()
    cells = float(ROWS * H * W)

    def total(k):
        value = acc[k]
        for d in range(ROWS - 1):
            value = value + peers[d, k]
        return jnp.sum(jnp.sum(value, axis=0, keepdims=True), axis=1, keepdims=True)

    base_rate = total(LEVELS + 1) / cells
    spread = 2.0 * base_rate * (1.0 - base_rate)
    lane = lax.broadcasted_iota(jnp.int32, (1, 8), 1)
    result = jnp.zeros((1, 8), F32)
    for k in range(LEVELS + 1):
        mean_error = total(k) * (MEMBERS / WEIGHTS[k]) / cells
        result = jnp.where(lane == k, 1.0 - mean_error * (LEVELS + 1) / spread, result)
    skill_ref[...] = result

    for copy in sends:
        copy.wait_send()


def on_device(predicted_surpass_tally, observed_surpass_tally):
    error = (predicted_surpass_tally[0] > 0).astype(F32) - (observed_surpass_tally > 0).astype(F32)
    vmem = pl.BlockSpec(memory_space=pltpu.VMEM)
    energy, skill = pl.pallas_call(
        kernel,
        out_shape=(
            jax.ShapeDtypeStruct((LEVELS + 1, H, 128), F32),
            jax.ShapeDtypeStruct((1, LEVELS + 1), F32),
        ),
        in_specs=[vmem, pl.BlockSpec(memory_space=pl.ANY)],
        out_specs=(vmem, vmem),
        scratch_shapes=[
            pltpu.VMEM((4, H, W), F32),
            pltpu.VMEM((5 * H, W), BF16),
            pltpu.VMEM((TILES, 2 * H, TILE), BF16),
            pltpu.VMEM((TILES, H, TILE), F32),
            pltpu.VMEM((LEVELS + 1, 2, SIDE, SIDE, H, 128), F32),
            pltpu.VMEM((LEVELS + 1, SIDE, SIDE, H, 128), F32),
            pltpu.VMEM((len(PIECES), 2, 6, SIDE, BLOCK, 128), F32),
            pltpu.VMEM((len(PIECES), 2, 6, BLOCK, 128), F32),
            pltpu.VMEM((2, 640 + 2 * PAD, 128), F32),
            pltpu.VMEM((LEVELS - 1, 2 * H, 384), BF16),
            pltpu.VMEM((2 * H, 640), BF16),
            pltpu.VMEM((2, 512 + 2 * PAD, 512), F32),
            pltpu.VMEM((2, 768 + 2 * PAD, TILE), F32),
            pltpu.VMEM((2, 768, TILE), BF16),
            pltpu.VMEM((2, 512, 512), BF16),
            pltpu.VMEM((H, 512), jnp.int32),
            pltpu.VMEM((LEVELS + 2, 8, 128), F32),
            pltpu.VMEM((ROWS - 1, LEVELS + 2, 8, 128), F32),
            pltpu.SemaphoreType.DMA,
            pltpu.SemaphoreType.DMA((len(HALO),)),
            pltpu.SemaphoreType.DMA((len(HALO),)),
            pltpu.SemaphoreType.DMA((len(PIECES), 28)),
            pltpu.SemaphoreType.DMA((len(PIECES), 28)),
            pltpu.SemaphoreType.DMA((ROWS - 1,)),
            pltpu.SemaphoreType.DMA((ROWS - 1,)),
        ],
        compiler_params=pltpu.CompilerParams(
            collective_id=0, has_side_effects=True, vmem_limit_bytes=67043328
        ),
    )(error, observed_surpass_tally)
    return energy[None], skill[None]


def solution(mesh):
    return jax.shard_map(
        on_device,
        mesh=mesh,
        in_specs=(P("mem", "row", None), P("row", None)),
        out_specs=(P(None, None, "row", "mem"), P("mem", None, None)),
        check_vma=False,
    )
```

```python
import functools

import jax
import jax.numpy as jnp
from jax import lax
from jax.experimental import pallas as pl
from jax.experimental.pallas import tpu as pltpu
from jax.sharding import PartitionSpec as P

MESH = pl.DeviceIdType.MESH
F32, BF16 = jnp.float32, jnp.bfloat16

LEVELS = 7
H = 128
W = 4096
TILE = 256
TILES = W // TILE
SIDE = 4
ROWS = 8
MEMBERS = 32
TAPS = (1.0 / 16.0, 4.0 / 16.0, 6.0 / 16.0, 4.0 / 16.0, 1.0 / 16.0)
WEIGHTS = [4.0 ** min(k + 1, LEVELS) for k in range(LEVELS + 1)]
PAD = 128
ROW_UNROLL, COL_UNROLL = 8, 7

SLOT_ROW = (128, 384, 0, 512)
HALO = (
    (0, 1, 112, 16),
    (1, -1, 0, 16),
    (0, 1, 64, 48),
    (1, -1, 16, 48),
    (0, 1, 0, 64),
    (1, -1, 64, 64),
    (2, 1, 64, 64),
    (3, -1, 0, 64),
    (2, 1, 32, 32),
    (3, -1, 64, 32),
    (2, 1, 0, 32),
    (3, -1, 96, 32),
)
OWN = 6
PIECES = [[(k, 0), (k, 32), (k, 64), (k, 96)] for k in range(6)]
PIECES += [[(6, 32), (6, 64), (7, 32), (7, 64)], [(6, 0), (6, 96), (7, 0), (7, 96)]]
BLOCK = 32
STRIP = 16
STRIPS = (7, 0, 6, 1, 5, 2, 4, 3)
DEPTH = 4


def kernel(
    pred_ref, obs_ref, out_ref, skill_ref,
    e_ref, pbuf, obuf, halo, ext, ub, sb, part, pair, ring1, ring2, xr, rm, rm7, xe, xi, ci, ce, acc, peers,
    psem, osem, zsend, zrecv, psend, precv, ksend, krecv,
):
    mem, row = lax.axis_index("mem"), lax.axis_index("row")
    c, y, x = lax.rem(mem, 2), lax.rem(mem // 2, SIDE), mem // (2 * SIDE)

    def at(xx, yy, cc):
        return (xx * SIDE + yy) * 2 + cc

    def along_z(step):
        return (mem, lax.rem(row + step + ROWS, ROWS))

    def along(axis, step):
        if axis == "y":
            return (at(x, lax.rem(y + step + SIDE, SIDE), c), row)
        return (at(lax.rem(x + step + SIDE, SIDE), y, c), row)

    sibling = (at(x, y, 1 - c), row)

    barrier = pltpu.get_barrier_semaphore()
    partners = [along_z(1), along_z(-1), sibling]
    partners += [along(axis, d) for axis in "xy" for d in (1, -1)]
    for partner in partners:
        pl.semaphore_signal(barrier, inc=1, device_id=partner, device_id_type=MESH)

    sends = []

    def remote(src, dst, send, recv, target):
        copy = pltpu.make_async_remote_copy(
            src_ref=src, dst_ref=dst, send_sem=send, recv_sem=recv, device_id=target, device_id_type=MESH
        )
        copy.start()
        sends.append(copy)
        return copy

    halos = {}

    def send_rows(n):
        slot, step, first, rows = HALO[n]
        span = pl.ds(first, rows)
        src = e_ref.at[span, :] if n < OWN else halo.at[slot - 2, span, :]
        halos[n] = remote(src, halo.at[slot, span, :], zsend.at[n], zrecv.at[n], along_z(step))

    def fetch(n):
        span = pl.ds(STRIPS[n] * STRIP, STRIP)
        slot = n % DEPTH
        return (
            pltpu.make_async_copy(pred_ref.at[span, :], pbuf.at[slot], psem.at[slot]),
            pltpu.make_async_copy(obs_ref.at[span, :], obuf.at[slot], osem.at[slot]),
        )

    acc[...] = jnp.zeros_like(acc)
    for n in range(DEPTH):
        for copy in fetch(n):
            copy.start()
    for n, strip in enumerate(STRIPS):
        for copy in fetch(n):
            copy.wait()
        first, slot = strip * STRIP, n % DEPTH

        @pl.loop(0, W // 512)
        def _(i):
            lanes = pl.ds(pl.multiple_of(i * 512, 512), 512)
            seen = jnp.where(obuf[slot, :, lanes] > 0, 1.0, 0.0)
            error = jnp.where(pbuf[slot, :, lanes] > 0, 1.0, 0.0) - seen
            e_ref[first : first + STRIP, lanes] = error
            ext[256 + first : 256 + first + STRIP, lanes] = error.astype(BF16)
            folded = seen[:, 0:128] + seen[:, 128:256] + seen[:, 256:384] + seen[:, 384:512]
            acc[LEVELS + 1] += jnp.sum(folded.reshape(STRIP // 8, 8, 128), axis=0)

        if n + DEPTH < len(STRIPS):
            for copy in fetch(n + DEPTH):
                copy.start()
        if n == 1:
            pl.semaphore_wait(barrier, len(partners))
            send_rows(0)
            send_rows(1)
    for n in range(2, OWN):
        send_rows(n)

    def arrive(*numbers):
        for n in numbers:
            halos[n].wait_recv()

    def take(n):
        slot, _, first, rows = HALO[n]

        @pl.loop(0, W // 512)
        def _(i):
            lanes = pl.ds(pl.multiple_of(i * 512, 512), 512)
            ext[SLOT_ROW[slot] + first : SLOT_ROW[slot] + first + rows, lanes] = halo[
                slot, first : first + rows, lanes
            ].astype(BF16)

    @pl.loop(0, W // 512)
    def _(i):
        lanes = pl.ds(pl.multiple_of(i * 512, 512), 512)
        for first, rows in ((0, 32), (128, 128), (384, 128), (608, 32)):
            ext[first : first + rows, lanes] = jnp.zeros((rows, 512), BF16)

    def taps(load, spacing):
        a, b, m, d, e = (load((q - 2) * spacing) for q in range(5))
        return TAPS[0] * (a + e) + TAPS[1] * (b + d) + TAPS[2] * m

    def split(value):
        high = value.astype(BF16)
        return high, (value - high.astype(F32)).astype(BF16)

    for side in range(2):
        xr[side, 0:PAD, :] = jnp.zeros((PAD, 128), F32)
        xr[side, PAD + 640 : 2 * PAD + 640, :] = jnp.zeros((PAD, 128), F32)
    for lane_block in range(5):
        index = lax.broadcasted_iota(jnp.int32, (640, 128), 0)
        domain = index + (row * H - 256)
        inside = (domain >= 0) & (domain < ROWS * H)
        lane = lax.broadcasted_iota(jnp.int32, (640, 128), 1) + lane_block * 128
        xr[0, PAD : PAD + 640, :] = jnp.where(inside & (index == lane), 1.0, 0.0)
        for level in range(1, LEVELS + 1):
            src, dst = (level + 1) % 2, level % 2
            new = taps(lambda o: xr[src, PAD + o : PAD + o + 640, :], 2 ** (level - 1))
            xr[dst, PAD : PAD + 640, :] = jnp.where(inside, new, 0.0)
            high, low = split(xr[dst, PAD + 256 : PAD + 384, :])
            if level == LEVELS:
                rm7[0:H, lane_block * 128 : lane_block * 128 + 128] = high
                rm7[H : 2 * H, lane_block * 128 : lane_block * 128 + 128] = low
            elif 1 <= lane_block <= 3:
                rm[level - 1, 0:H, lane_block * 128 - 128 : lane_block * 128] = high
                rm[level - 1, H : 2 * H, lane_block * 128 - 128 : lane_block * 128] = low

    for side in range(2):
        for start in (0, PAD + 768):
            xi[side, start : start + PAD, :] = jnp.zeros((PAD, TILE), F32)
        for start in (0, PAD + 512):
            xe[side, start : start + PAD, :] = jnp.zeros((PAD, 512), F32)
    xi[0, PAD : PAD + 768, :] = jnp.where(
        lax.broadcasted_iota(jnp.int32, (768, TILE), 0) - 256 == lax.broadcasted_iota(jnp.int32, (768, TILE), 1),
        1.0, 0.0,
    )
    xe[0, PAD : PAD + 512, :] = jnp.where(
        lax.broadcasted_iota(jnp.int32, (512, 512), 0) == lax.broadcasted_iota(jnp.int32, (512, 512), 1), 1.0, 0.0
    )

    def column_operators(level):
        src, dst = (level + 1) % 2, level % 2
        spacing = 2 ** (level - 1)

        @pl.loop(0, TILE // 128)
        def _(i):
            lanes = pl.ds(pl.multiple_of(i * 128, 128), 128)
            new = taps(lambda o: xi[src, PAD + o : PAD + o + 768, lanes], spacing)
            xi[dst, PAD : PAD + 768, lanes] = new
            ci[0, :, lanes], ci[1, :, lanes] = split(new)

        @pl.loop(0, 512 // 128)
        def _(i):
            lanes = pl.ds(pl.multiple_of(i * 128, 128), 128)
            new = taps(lambda o: xe[src, PAD + o : PAD + o + 512, lanes], spacing)
            xe[dst, PAD : PAD + 512, lanes] = new
            ce[0, :, lanes], ce[1, :, lanes] = split(new)

    def level_pass(level, spans):
        reach = 256 if level == LEVELS else 128
        height = sum(rows for _, rows in spans)
        ops = rm7 if level == LEVELS else rm.at[level - 1]
        depth = slice(0, 640) if level == LEVELS else slice(128, 512)

        def pick(ref, offset):
            return [ref[offset + first : offset + first + rows, :] for first, rows in spans]

        @pl.loop(0, TILES, unroll=ROW_UNROLL)
        def _(t):
            lanes = pl.ds(pl.multiple_of(t * TILE, TILE), TILE)
            left = jnp.concatenate(pick(ops, 0) + pick(ops, H), axis=0)
            both = jnp.dot(left, ext[depth, lanes], preferred_element_type=F32)
            high, low = split(both[:height] + both[height:])
            done = 0
            for first, rows in spans:
                ub[t, first : first + rows, :] = high[done : done + rows]
                ub[t, H + first : H + first + rows, :] = low[done : done + rows]
                done += rows

        def finish(t, both, cross):
            smooth = both[:height] + both[height:] + cross
            lanes = pl.ds(pl.multiple_of(t * TILE, TILE), TILE) if not isinstance(t, int) else pl.ds(t * TILE, TILE)
            done = 0
            for first, rows in spans:
                now = smooth[done : done + rows]
                before = e_ref[first : first + rows, lanes] if level == 1 else sb[t, first : first + rows, :]
                store(level - 1, t, first, rows, before - now)
                if level == LEVELS:
                    store(LEVELS, t, first, rows, now)
                else:
                    sb[t, first : first + rows, :] = now
                done += rows

        def store(k, t, first, rows, component):
            energy = component * component * (WEIGHTS[k] / MEMBERS)
            for core in range(2):
                part[k, core, t // SIDE, t % SIDE, first : first + rows, :] = energy[:, core * 128 : core * 128 + 128]
            folded = energy[:, 0:128] + energy[:, 128:256]
            acc[k] += jnp.sum(folded.reshape(rows // 8, 8, 128), axis=0)

        def lhs(tiles):
            return jnp.concatenate(
                [
                    jnp.concatenate(
                        [ub[t, offset + first : offset + first + rows, lanes] for t, lanes in tiles], axis=1
                    )
                    for offset in (0, H)
                    for first, rows in spans
                ],
                axis=0,
            )

        near_left, whole, near_right = slice(256 - reach, 256), slice(0, 256), slice(0, reach)

        @pl.loop(1, TILES - 1, unroll=COL_UNROLL)
        def _(t):
            left = lhs([(t - 1, near_left), (t, whole), (t + 1, near_right)])
            depth = slice(256 - reach, 512 + reach)
            both = jnp.dot(left, ci[0, depth, :], preferred_element_type=F32)
            cross = jnp.dot(left[:height], ci[1, depth, :], preferred_element_type=F32)
            finish(t, both, cross)

        for t, tiles, out, depth in (
            (0, [(0, whole), (1, near_right)], slice(0, 256), slice(0, 256 + reach)),
            (TILES - 1, [(TILES - 2, near_left), (TILES - 1, whole)], slice(256, 512), slice(256 - reach, 512)),
        ):
            left = lhs(tiles)
            dims = (((1,), (1,)), ((), ()))
            both = lax.dot_general(left, ce[0, out, depth], dims, preferred_element_type=F32)
            cross = lax.dot_general(left[:height], ce[1, out, depth], dims, preferred_element_type=F32)
            finish(t, both, cross)

    flights = {}

    def block_of(p, i, axis, pos, stage):
        k, first = PIECES[p][i]
        rows = pl.ds(first, BLOCK)
        if stage == 1:
            if axis == "y":
                return part.at[k, c, :, pos, rows, :]
            return part.at[k, c, pos, :, rows, :]
        if axis == "y":
            return part.at[k, c, x, pos, rows, :]
        return part.at[k, c, pos, y, rows, :]

    def axis_of(half, stage):
        return "yx"[(half + stage - 1) % 2]

    def spot(axis, step):
        return lax.rem((y if axis == "y" else x) + step + SIDE, SIDE)

    def pair_start(p):
        for i, (k, first) in enumerate(PIECES[p]):
            rows = pl.ds(first, BLOCK)
            flights[p, 0, i] = remote(
                part.at[k, 1 - c, :, :, rows, :], pair.at[k, :, :, rows, :], psend.at[p, i], precv.at[p, i], sibling
            )

    def ring_copy(p, stage, half, n, i, pos, step):
        axis = axis_of(half, stage)
        landing = (ring1 if stage == 1 else ring2).at[p, half, n]
        sem = 4 + (stage - 1) * 12 + half * 6 + n
        flights[p, stage, half, n] = remote(
            block_of(p, i, axis, spot(axis, pos), stage), landing, psend.at[p, sem], precv.at[p, sem], along(axis, step)
        )

    def ring_start(p, stage):
        for half in range(2):
            i0, i1 = 2 * half, 2 * half + 1
            ring_copy(p, stage, half, 0, i0, 2, 1)
            ring_copy(p, stage, half, 1, i1, 2, -1)
            ring_copy(p, stage, half, 2, i1, 1, 1)
            ring_copy(p, stage, half, 3, i0, -1, -1)

    def ring_add(p, stage, half, n, i, pos):
        axis = axis_of(half, stage)
        flights[p, stage, half, n].wait_recv()
        block = block_of(p, i, axis, spot(axis, pos), stage)
        block[...] = block[...] + (ring1 if stage == 1 else ring2)[p, half, n]

    def ring_middle(p, stage):
        for half in range(2):
            i0, i1 = 2 * half, 2 * half + 1
            ring_add(p, stage, half, 0, i0, 1)
            ring_copy(p, stage, half, 4, i0, 1, 1)
            ring_add(p, stage, half, 1, i1, -1)
            ring_copy(p, stage, half, 5, i1, -1, -1)

    def ring_end(p, stage):
        for half in range(2):
            i0, i1 = 2 * half, 2 * half + 1
            ring_add(p, stage, half, 3, i0, 0)
            ring_add(p, stage, half, 2, i1, 0)
            ring_add(p, stage, half, 4, i0, 0)
            ring_add(p, stage, half, 5, i1, 0)

    def advance(p, step):
        if step == 0:
            pair_start(p)
        elif step == 1:
            for i, (k, first) in enumerate(PIECES[p]):
                flights[p, 0, i].wait_recv()

                @pl.loop(0, SIDE)
                def _(j):
                    rows = pl.ds(first, BLOCK)
                    part[k, c, j, :, rows, :] = part[k, c, j, :, rows, :] + pair[k, j, :, rows, :]

            ring_start(p, 1)
        elif step == 2:
            ring_middle(p, 1)
        elif step == 3:
            ring_end(p, 1)
            ring_start(p, 2)
        elif step == 4:
            ring_middle(p, 2)
        elif step == 5:
            ring_end(p, 2)
            for k, first in PIECES[p]:
                out_ref[k, first : first + BLOCK, :] = part[k, c, x, y, pl.ds(first, BLOCK), :]

    position = {}

    def tick(limit):
        for p in sorted(position):
            if p <= limit and position[p] < 5:
                position[p] += 1
                advance(p, position[p])

    def begin(p):
        position[p] = 0
        advance(p, 0)

    everything = [(0, H)]
    for level in range(1, LEVELS):
        column_operators(level)
        if level == 1:
            arrive(0, 1)
            take(0), take(1)
        if level == 3:
            arrive(2, 3)
            send_rows(6), send_rows(7)
            take(2), take(3)
        if level == 5:
            arrive(4, 5)
            for n in range(8, 12):
                send_rows(n)
            take(4), take(5)
        level_pass(level, everything)
        tick(level - 2)
        begin(level - 1)

    column_operators(LEVELS)
    while any(position[p] < 5 for p in range(6)):
        tick(5)

    arrive(6, 7, 8, 9)
    take(6), take(7), take(8), take(9)
    level_pass(LEVELS, [(32, 64)])
    begin(6)
    tick(6)
    tick(6)
    arrive(10, 11)
    take(10), take(11)
    level_pass(LEVELS, [(0, 32), (96, 32)])
    begin(7)

    def relay(hop):
        for step in (1, -1):
            if step == -1 and hop == ROWS // 2:
                continue
            if hop > 1:
                flights["tally", hop - 1, step].wait_recv()
            src = acc if hop == 1 else peers.at[(step * (hop - 1)) % ROWS]
            slot = (step * hop) % ROWS
            flights["tally", hop, step] = remote(src, peers.at[slot], ksend.at[slot], krecv.at[slot], along_z(step))

    hop = 0
    while any(position[p] < 5 for p in position) or hop < ROWS // 2:
        if hop < ROWS // 2:
            hop += 1
            relay(hop)
        tick(7)
    flights["tally", ROWS // 2, 1].wait_recv()
    flights["tally", ROWS // 2 - 1, -1].wait_recv()
    cells = float(ROWS * H * W)

    def total(k):
        value = acc[k]
        for d in range(1, ROWS):
            value = value + peers[d, k]
        return jnp.sum(jnp.sum(value, axis=0, keepdims=True), axis=1, keepdims=True)

    base_rate = total(LEVELS + 1) / cells
    spread = 2.0 * base_rate * (1.0 - base_rate)
    lane = lax.broadcasted_iota(jnp.int32, (1, 8), 1)
    result = jnp.zeros((1, 8), F32)
    for k in range(LEVELS + 1):
        mean_error = total(k) * (MEMBERS / WEIGHTS[k]) / cells
        result = jnp.where(lane == k, 1.0 - mean_error * (LEVELS + 1) / spread, result)
    skill_ref[...] = result

    for copy in sends:
        copy.wait_send()


def on_device(predicted_surpass_tally, observed_surpass_tally):
    vmem = pl.BlockSpec(memory_space=pltpu.VMEM)
    energy, skill = pl.pallas_call(
        kernel,
        out_shape=(
            jax.ShapeDtypeStruct((LEVELS + 1, H, 128), F32),
            jax.ShapeDtypeStruct((1, LEVELS + 1), F32),
        ),
        in_specs=[pl.BlockSpec(memory_space=pl.ANY)] * 2,
        out_specs=(vmem, vmem),
        scratch_shapes=[
            pltpu.VMEM((H, W), F32),
            pltpu.VMEM((DEPTH, STRIP, W), jnp.int32),
            pltpu.VMEM((DEPTH, STRIP, W), jnp.int32),
            pltpu.VMEM((4, H, W), F32),
            pltpu.VMEM((5 * H, W), BF16),
            pltpu.VMEM((TILES, 2 * H, TILE), BF16),
            pltpu.VMEM((TILES, H, TILE), F32),
            pltpu.VMEM((LEVELS + 1, 2, SIDE, SIDE, H, 128), F32),
            pltpu.VMEM((LEVELS + 1, SIDE, SIDE, H, 128), F32),
            pltpu.VMEM((len(PIECES), 2, 6, SIDE, BLOCK, 128), F32),
            pltpu.VMEM((len(PIECES), 2, 6, BLOCK, 128), F32),
            pltpu.VMEM((2, 640 + 2 * PAD, 128), F32),
            pltpu.VMEM((LEVELS - 1, 2 * H, 384), BF16),
            pltpu.VMEM((2 * H, 640), BF16),
            pltpu.VMEM((2, 512 + 2 * PAD, 512), F32),
            pltpu.VMEM((2, 768 + 2 * PAD, TILE), F32),
            pltpu.VMEM((2, 768, TILE), BF16),
            pltpu.VMEM((2, 512, 512), BF16),
            pltpu.VMEM((LEVELS + 2, 8, 128), F32),
            pltpu.VMEM((ROWS, LEVELS + 2, 8, 128), F32),
            pltpu.SemaphoreType.DMA((DEPTH,)),
            pltpu.SemaphoreType.DMA((DEPTH,)),
            pltpu.SemaphoreType.DMA((len(HALO),)),
            pltpu.SemaphoreType.DMA((len(HALO),)),
            pltpu.SemaphoreType.DMA((len(PIECES), 28)),
            pltpu.SemaphoreType.DMA((len(PIECES), 28)),
            pltpu.SemaphoreType.DMA((ROWS,)),
            pltpu.SemaphoreType.DMA((ROWS,)),
        ],
        compiler_params=pltpu.CompilerParams(
            collective_id=0, has_side_effects=True, vmem_limit_bytes=67043328
        ),
    )(predicted_surpass_tally[0], observed_surpass_tally)
    return energy[None], skill[None]


def solution(mesh):
    return jax.shard_map(
        on_device,
        mesh=mesh,
        in_specs=(P("mem", "row", None), P("row", None)),
        out_specs=(P(None, None, "row", "mem"), P("mem", None, None)),
        check_vma=False,
    )
```

```python
import functools

import jax
import jax.numpy as jnp
from jax import lax
from jax.experimental import pallas as pl
from jax.experimental.pallas import tpu as pltpu
from jax.sharding import PartitionSpec as P

MESH = pl.DeviceIdType.MESH
F32, BF16 = jnp.float32, jnp.bfloat16

LEVELS = 7
H = 128
W = 4096
TILE = 256
TILES = W // TILE
SIDE = 4
ROWS = 8
MEMBERS = 32
TAPS = (1.0 / 16.0, 4.0 / 16.0, 6.0 / 16.0, 4.0 / 16.0, 1.0 / 16.0)
WEIGHTS = [4.0 ** min(k + 1, LEVELS) for k in range(LEVELS + 1)]
PAD = 128
ROW_UNROLL = 8
STACK = (1, 1, 1, 1, 1, 1, 1, 7, 7)

SLOT_ROW = (128, 384, 0, 512)
HALO = (
    (0, 1, 112, 16),
    (1, -1, 0, 16),
    (0, 1, 64, 48),
    (1, -1, 16, 48),
    (0, 1, 0, 64),
    (1, -1, 64, 64),
    (2, 1, 64, 64),
    (3, -1, 0, 64),
    (2, 1, 32, 32),
    (3, -1, 64, 32),
    (2, 1, 16, 16),
    (3, -1, 96, 16),
    (2, 1, 0, 16),
    (3, -1, 112, 16),
)
OWN = 6
PIECES = [(32, [(k, 0), (k, 32), (k, 64), (k, 96)]) for k in range(6)]
PIECES += [
    (32, [(6, 32), (6, 64), (7, 32), (7, 64)]),
    (16, [(6, 16), (6, 96), (7, 16), (7, 96)]),
    (16, [(6, 0), (6, 112), (7, 0), (7, 112)]),
]
BLOCK = 32
STRIP = 16
STRIPS = (7, 0, 6, 1, 5, 2, 4, 3)
DEPTH = 2


def kernel(
    pred_ref, obs_ref, out_ref, skill_ref,
    e_ref, pbuf, obuf, halo, ext, ub, sb, part, pair, ring1, ring2, xr, rm, rm7, xe, xi, ci, ce, acc, peers,
    psem, osem, zsend, zrecv, psend, precv, ksend, krecv,
):
    mem, row = lax.axis_index("mem"), lax.axis_index("row")
    c, y, x = lax.rem(mem, 2), lax.rem(mem // 2, SIDE), mem // (2 * SIDE)

    def at(xx, yy, cc):
        return (xx * SIDE + yy) * 2 + cc

    def along_z(step):
        return (mem, lax.rem(row + step + ROWS, ROWS))

    def along(axis, step):
        if axis == "y":
            return (at(x, lax.rem(y + step + SIDE, SIDE), c), row)
        return (at(lax.rem(x + step + SIDE, SIDE), y, c), row)

    sibling = (at(x, y, 1 - c), row)

    barrier = pltpu.get_barrier_semaphore()
    partners = [along_z(1), along_z(-1), sibling]
    partners += [along(axis, d) for axis in "xy" for d in (1, -1)]
    for partner in partners:
        pl.semaphore_signal(barrier, inc=1, device_id=partner, device_id_type=MESH)

    sends = []

    def remote(src, dst, send, recv, target):
        copy = pltpu.make_async_remote_copy(
            src_ref=src, dst_ref=dst, send_sem=send, recv_sem=recv, device_id=target, device_id_type=MESH
        )
        copy.start()
        sends.append(copy)
        return copy

    halos = {}

    def send_rows(n):
        slot, step, first, rows = HALO[n]
        span = pl.ds(first, rows)
        src = e_ref.at[span, :] if n < OWN else halo.at[slot - 2, span, :]
        halos[n] = remote(src, halo.at[slot, span, :], zsend.at[n], zrecv.at[n], along_z(step))

    def fetch(n):
        span = pl.ds(STRIPS[n] * STRIP, STRIP)
        slot = n % DEPTH
        return (
            pltpu.make_async_copy(pred_ref.at[span, :], pbuf.at[slot], psem.at[slot]),
            pltpu.make_async_copy(obs_ref.at[span, :], obuf.at[slot], osem.at[slot]),
        )

    acc[...] = jnp.zeros_like(acc)
    for n in range(DEPTH):
        for copy in fetch(n):
            copy.start()
    for n, strip in enumerate(STRIPS):
        for copy in fetch(n):
            copy.wait()
        first, slot = strip * STRIP, n % DEPTH

        @pl.loop(0, W // 512)
        def _(i):
            lanes = pl.ds(pl.multiple_of(i * 512, 512), 512)
            seen = jnp.where(obuf[slot, :, lanes] > 0, 1.0, 0.0)
            error = jnp.where(pbuf[slot, :, lanes] > 0, 1.0, 0.0) - seen
            e_ref[first : first + STRIP, lanes] = error
            ext[256 + first : 256 + first + STRIP, lanes] = error.astype(BF16)
            folded = seen[:, 0:128] + seen[:, 128:256] + seen[:, 256:384] + seen[:, 384:512]
            acc[LEVELS + 1] += jnp.sum(folded.reshape(STRIP // 8, 8, 128), axis=0)

        if n + DEPTH < len(STRIPS):
            for copy in fetch(n + DEPTH):
                copy.start()
        if n == 1:
            pl.semaphore_wait(barrier, len(partners))
            send_rows(0)
            send_rows(1)
    for n in range(2, OWN):
        send_rows(n)

    def arrive(*numbers):
        for n in numbers:
            halos[n].wait_recv()

    def take(n):
        slot, _, first, rows = HALO[n]

        @pl.loop(0, W // 512)
        def _(i):
            lanes = pl.ds(pl.multiple_of(i * 512, 512), 512)
            ext[SLOT_ROW[slot] + first : SLOT_ROW[slot] + first + rows, lanes] = halo[
                slot, first : first + rows, lanes
            ].astype(BF16)

    @pl.loop(0, W // 512)
    def _(i):
        lanes = pl.ds(pl.multiple_of(i * 512, 512), 512)
        for first, rows in ((0, 32), (128, 128), (384, 128), (608, 32)):
            ext[first : first + rows, lanes] = jnp.zeros((rows, 512), BF16)

    def taps(load, spacing):
        a, b, m, d, e = (load((q - 2) * spacing) for q in range(5))
        return TAPS[0] * (a + e) + TAPS[1] * (b + d) + TAPS[2] * m

    def split(value):
        high = value.astype(BF16)
        return high, (value - high.astype(F32)).astype(BF16)

    for side in range(2):
        xr[side, 0:PAD, :] = jnp.zeros((PAD, 128), F32)
        xr[side, PAD + 640 : 2 * PAD + 640, :] = jnp.zeros((PAD, 128), F32)
    for lane_block in range(5):
        index = lax.broadcasted_iota(jnp.int32, (640, 128), 0)
        domain = index + (row * H - 256)
        inside = (domain >= 0) & (domain < ROWS * H)
        lane = lax.broadcasted_iota(jnp.int32, (640, 128), 1) + lane_block * 128
        xr[0, PAD : PAD + 640, :] = jnp.where(inside & (index == lane), 1.0, 0.0)
        for level in range(1, LEVELS + 1):
            src, dst = (level + 1) % 2, level % 2
            new = taps(lambda o: xr[src, PAD + o : PAD + o + 640, :], 2 ** (level - 1))
            xr[dst, PAD : PAD + 640, :] = jnp.where(inside, new, 0.0)
            high, low = split(xr[dst, PAD + 256 : PAD + 384, :])
            if level == LEVELS:
                rm7[0:H, lane_block * 128 : lane_block * 128 + 128] = high
                rm7[H : 2 * H, lane_block * 128 : lane_block * 128 + 128] = low
            elif 1 <= lane_block <= 3:
                rm[level - 1, 0:H, lane_block * 128 - 128 : lane_block * 128] = high
                rm[level - 1, H : 2 * H, lane_block * 128 - 128 : lane_block * 128] = low

    for side in range(2):
        for start in (0, PAD + 768):
            xi[side, start : start + PAD, :] = jnp.zeros((PAD, TILE), F32)
        for start in (0, PAD + 512):
            xe[side, start : start + PAD, :] = jnp.zeros((PAD, 512), F32)
    xi[0, PAD : PAD + 768, :] = jnp.where(
        lax.broadcasted_iota(jnp.int32, (768, TILE), 0) - 256 == lax.broadcasted_iota(jnp.int32, (768, TILE), 1),
        1.0, 0.0,
    )
    xe[0, PAD : PAD + 512, :] = jnp.where(
        lax.broadcasted_iota(jnp.int32, (512, 512), 0) == lax.broadcasted_iota(jnp.int32, (512, 512), 1), 1.0, 0.0
    )

    def column_operators(level):
        src, dst = (level + 1) % 2, level % 2
        spacing = 2 ** (level - 1)

        @pl.loop(0, TILE // 128)
        def _(i):
            lanes = pl.ds(pl.multiple_of(i * 128, 128), 128)
            new = taps(lambda o: xi[src, PAD + o : PAD + o + 768, lanes], spacing)
            xi[dst, PAD : PAD + 768, lanes] = new
            ci[0, :, lanes], ci[1, :, lanes] = split(new)

        @pl.loop(0, 512 // 128)
        def _(i):
            lanes = pl.ds(pl.multiple_of(i * 128, 128), 128)
            new = taps(lambda o: xe[src, PAD + o : PAD + o + 512, lanes], spacing)
            xe[dst, PAD : PAD + 512, lanes] = new
            ce[0, :, lanes], ce[1, :, lanes] = split(new)

    def pair_copy(p, i, group):
        height, blocks = PIECES[p]
        k, first = blocks[i]
        half = pl.ds(group * (SIDE // 2), SIDE // 2)
        rows = pl.ds(first, height)
        return pltpu.make_async_remote_copy(
            src_ref=part.at[k, 1 - c, half, :, rows, :],
            dst_ref=pair.at[k, half, :, rows, :],
            send_sem=psend.at[p, 2 * i + group],
            recv_sem=precv.at[p, 2 * i + group],
            device_id=sibling,
            device_id_type=MESH,
        )

    def level_pass(level, spans, piece):
        reach = 256 if level == LEVELS else 128
        height = sum(rows for _, rows in spans)
        ops = rm7 if level == LEVELS else rm.at[level - 1]
        depth = slice(0, 640) if level == LEVELS else slice(128, 512)
        late = piece > 6
        stack = STACK[piece]

        def pick(ref, offset):
            return [ref[offset + first : offset + first + rows, :] for first, rows in spans]

        @pl.loop(0, TILES, unroll=ROW_UNROLL)
        def _(t):
            lanes = pl.ds(pl.multiple_of(t * TILE, TILE), TILE)
            if late:
                left = jnp.concatenate(pick(ops, 0) + pick(ops, H), axis=0)
                left = jnp.concatenate([left[:, 0:32], left[:, 608:640]], axis=1)
                right = jnp.concatenate([ext[0:32, lanes], ext[608:640, lanes]], axis=0)
            else:
                left, right = ops[...], ext[depth, lanes]
            both = jnp.dot(left, right, preferred_element_type=F32)
            value = both[: left.shape[0] // 2] + both[left.shape[0] // 2 :]
            if late:
                value = value + jnp.concatenate(
                    [
                        jnp.concatenate(
                            [part[LEVELS, core, t // SIDE, t % SIDE, first : first + rows, :] for core in range(2)], axis=1
                        )
                        for first, rows in spans
                    ],
                    axis=0,
                )
            elif piece == 6:
                for first in (0, 96):
                    for core in range(2):
                        part[LEVELS, core, t // SIDE, t % SIDE, first : first + 32, :] = value[
                            first : first + 32, core * 128 : core * 128 + 128
                        ]
                value = value[32:96]
            high, low = split(value)
            done = 0
            for first, rows in spans:
                ub[t, first : first + rows, :] = high[done : done + rows]
                ub[t, H + first : H + first + rows, :] = low[done : done + rows]
                done += rows

        def finish(t, both, cross):
            smooth = both[:height] + both[height:] + cross
            lanes = pl.ds(pl.multiple_of(t * TILE, TILE), TILE) if not isinstance(t, int) else pl.ds(t * TILE, TILE)
            done = 0
            for first, rows in spans:
                now = smooth[done : done + rows]
                before = e_ref[first : first + rows, lanes] if level == 1 else sb[t, first : first + rows, :]
                store(level - 1, t, first, rows, before - now)
                if level == LEVELS:
                    store(LEVELS, t, first, rows, now)
                else:
                    sb[t, first : first + rows, :] = now
                done += rows

        def store(k, t, first, rows, component):
            energy = component * component * (WEIGHTS[k] / MEMBERS)
            for core in range(2):
                part[k, core, t // SIDE, t % SIDE, first : first + rows, :] = energy[:, core * 128 : core * 128 + 128]
            folded = energy[:, 0:128] + energy[:, 128:256]
            acc[k] += jnp.sum(folded.reshape(rows // 8, 8, 128), axis=0)

        def lhs(tiles):
            return jnp.concatenate(
                [
                    jnp.concatenate(
                        [ub[t, offset + first : offset + first + rows, lanes] for t, lanes in tiles], axis=1
                    )
                    for offset in (0, H)
                    for first, rows in spans
                ],
                axis=0,
            )

        near_left, whole, near_right = slice(256 - reach, 256), slice(0, 256), slice(0, reach)

        for t, tiles, out, depth in (
            (0, [(0, whole), (1, near_right)], slice(0, 256), slice(0, 256 + reach)),
            (TILES - 1, [(TILES - 2, near_left), (TILES - 1, whole)], slice(256, 512), slice(256 - reach, 512)),
        ):
            left = lhs(tiles)
            dims = (((1,), (1,)), ((), ()))
            both = lax.dot_general(left, ce[0, out, depth], dims, preferred_element_type=F32)
            cross = lax.dot_general(left[:height], ce[1, out, depth], dims, preferred_element_type=F32)
            finish(t, both, cross)

        @pl.loop(0, 2)
        def _(group):
            depth = slice(256 - reach, 512 + reach)
            for j in range(0, TILES // 2 - 1, stack):
                tiles = [group * (TILES // 2 - 1) + (j + n + 1) for n in range(stack)]
                parts = [lhs([(t - 1, near_left), (t, whole), (t + 1, near_right)]) for t in tiles]
                left = jnp.concatenate(parts, axis=0)
                both = jnp.dot(left, ci[0, depth, :], preferred_element_type=F32)
                left = jnp.concatenate([one[:height] for one in parts], axis=0)
                cross = jnp.dot(left, ci[1, depth, :], preferred_element_type=F32)
                for n, t in enumerate(tiles):
                    finish(t, both[2 * n * height : 2 * (n + 1) * height], cross[n * height : (n + 1) * height])
            for i in range(4):
                pair_copy(piece, i, group).start()

    flights = {}

    def block_of(p, i, axis, pos, stage):
        height, blocks = PIECES[p]
        k, first = blocks[i]
        rows = pl.ds(first, height)
        if stage == 1:
            if axis == "y":
                return part.at[k, c, :, pos, rows, :]
            return part.at[k, c, pos, :, rows, :]
        if axis == "y":
            return part.at[k, c, x, pos, rows, :]
        return part.at[k, c, pos, y, rows, :]

    def axis_of(half, stage):
        return "yx"[(half + stage - 1) % 2]

    def spot(axis, step):
        return lax.rem((y if axis == "y" else x) + step + SIDE, SIDE)

    def ring_copy(p, stage, half, n, i, pos, step):
        axis = axis_of(half, stage)
        height = PIECES[p][0]
        slot, base = (p, 0) if p < 8 else (p - 1, height)
        if stage == 1:
            landing = ring1.at[slot, half, n, :, pl.ds(base, height), :]
        else:
            landing = ring2.at[slot, half, n, pl.ds(base, height), :]
        sem = 8 + (stage - 1) * 12 + half * 6 + n
        flights[p, stage, half, n] = remote(
            block_of(p, i, axis, spot(axis, pos), stage), landing, psend.at[p, sem], precv.at[p, sem], along(axis, step)
        )

    def ring_start(p, stage, i):
        half = i // 2
        if i % 2 == 0:
            ring_copy(p, stage, half, 0, i, 2, 1)
            ring_copy(p, stage, half, 3, i, -1, -1)
        else:
            ring_copy(p, stage, half, 1, i, 2, -1)
            ring_copy(p, stage, half, 2, i, 1, 1)

    def ring_add(p, stage, half, n, i, pos):
        axis = axis_of(half, stage)
        flights[p, stage, half, n].wait_recv()
        block = block_of(p, i, axis, spot(axis, pos), stage)
        height = PIECES[p][0]
        slot, base = (p, 0) if p < 8 else (p - 1, height)
        if stage == 1:
            block[...] = block[...] + ring1[slot, half, n, :, base : base + height, :]
        else:
            block[...] = block[...] + ring2[slot, half, n, base : base + height, :]

    def ring_middle(p, stage):
        for half in range(2):
            i0, i1 = 2 * half, 2 * half + 1
            ring_add(p, stage, half, 0, i0, 1)
            ring_copy(p, stage, half, 4, i0, 1, 1)
            ring_add(p, stage, half, 1, i1, -1)
            ring_copy(p, stage, half, 5, i1, -1, -1)

    def ring_end(p, stage, i):
        half = i // 2
        ring_add(p, stage, half, 3 if i % 2 == 0 else 2, i, 0)
        ring_add(p, stage, half, 4 if i % 2 == 0 else 5, i, 0)

    def advance(p, step):
        height, blocks = PIECES[p]
        if step == 1:
            for i, (k, first) in enumerate(blocks):
                rows = pl.ds(first, height)
                for group in range(2):
                    copy = pair_copy(p, i, group)
                    copy.wait_recv()
                    sends.append(copy)

                    @pl.loop(2 * group, 2 * group + 2)
                    def _(j):
                        part[k, c, j, :, rows, :] = part[k, c, j, :, rows, :] + pair[k, j, :, rows, :]

                ring_start(p, 1, i)
        elif step == 2:
            ring_middle(p, 1)
        elif step == 3:
            for i in range(4):
                ring_end(p, 1, i)
                ring_start(p, 2, i)
        elif step == 4:
            ring_middle(p, 2)
        elif step == 5:
            for i, (k, first) in enumerate(blocks):
                ring_end(p, 2, i)
                out_ref[k, first : first + height, :] = part[k, c, x, y, pl.ds(first, height), :]

    position = {}

    def tick(limit):
        for p in sorted(position):
            if p <= limit and position[p] < 5:
                position[p] += 1
                advance(p, position[p])

    everything = [(0, H)]
    for level in range(1, LEVELS):
        column_operators(level)
        if level == 1:
            arrive(0, 1)
            take(0), take(1)
        if level == 3:
            arrive(2, 3)
            send_rows(6), send_rows(7)
            take(2), take(3)
        if level == 5:
            arrive(4, 5)
            for n in range(8, len(HALO)):
                send_rows(n)
            take(4), take(5)
        level_pass(level, everything, level - 1)
        tick(level - 2)
        position[level - 1] = 0

    column_operators(LEVELS)
    while any(position[p] < 5 for p in range(6)):
        tick(5)

    arrive(6, 7, 8, 9)
    take(6), take(7), take(8), take(9)
    level_pass(LEVELS, [(32, 64)], 6)
    position[6] = 0
    tick(6)
    arrive(10, 11)
    take(10), take(11)
    level_pass(LEVELS, [(16, 16), (96, 16)], 7)
    position[7] = 0
    tick(7)
    arrive(12, 13)
    take(12), take(13)
    level_pass(LEVELS, [(0, 16), (112, 16)], 8)
    position[8] = 0

    def relay(hop):
        for step in (1, -1):
            if step == -1 and hop == ROWS // 2:
                continue
            if hop > 1:
                flights["tally", hop - 1, step].wait_recv()
            src = acc if hop == 1 else peers.at[(step * (hop - 1)) % ROWS]
            slot = (step * hop) % ROWS
            flights["tally", hop, step] = remote(src, peers.at[slot], ksend.at[slot], krecv.at[slot], along_z(step))

    hop = 0
    while any(position[p] < 5 for p in position) or hop < ROWS // 2:
        if hop < ROWS // 2:
            hop += 1
            relay(hop)
        tick(8)
    flights["tally", ROWS // 2, 1].wait_recv()
    flights["tally", ROWS // 2 - 1, -1].wait_recv()
    cells = float(ROWS * H * W)

    def total(k):
        value = acc[k]
        for d in range(1, ROWS):
            value = value + peers[d, k]
        return jnp.sum(jnp.sum(value, axis=0, keepdims=True), axis=1, keepdims=True)

    base_rate = total(LEVELS + 1) / cells
    spread = 2.0 * base_rate * (1.0 - base_rate)
    lane = lax.broadcasted_iota(jnp.int32, (1, 8), 1)
    result = jnp.zeros((1, 8), F32)
    for k in range(LEVELS + 1):
        mean_error = total(k) * (MEMBERS / WEIGHTS[k]) / cells
        result = jnp.where(lane == k, 1.0 - mean_error * (LEVELS + 1) / spread, result)
    skill_ref[...] = result

    for copy in sends:
        copy.wait_send()


def on_device(predicted_surpass_tally, observed_surpass_tally):
    vmem = pl.BlockSpec(memory_space=pltpu.VMEM)
    energy, skill = pl.pallas_call(
        kernel,
        out_shape=(
            jax.ShapeDtypeStruct((LEVELS + 1, H, 128), F32),
            jax.ShapeDtypeStruct((1, LEVELS + 1), F32),
        ),
        in_specs=[pl.BlockSpec(memory_space=pl.ANY)] * 2,
        out_specs=(vmem, vmem),
        scratch_shapes=[
            pltpu.VMEM((H, W), F32),
            pltpu.VMEM((DEPTH, STRIP, W), jnp.int32),
            pltpu.VMEM((DEPTH, STRIP, W), jnp.int32),
            pltpu.VMEM((4, H, W), F32),
            pltpu.VMEM((5 * H, W), BF16),
            pltpu.VMEM((TILES, 2 * H, TILE), BF16),
            pltpu.VMEM((TILES, H, TILE), F32),
            pltpu.VMEM((LEVELS + 1, 2, SIDE, SIDE, H, 128), F32),
            pltpu.VMEM((LEVELS + 1, SIDE, SIDE, H, 128), F32),
            pltpu.VMEM((len(PIECES) - 1, 2, 6, SIDE, BLOCK, 128), F32),
            pltpu.VMEM((len(PIECES) - 1, 2, 6, BLOCK, 128), F32),
            pltpu.VMEM((2, 640 + 2 * PAD, 128), F32),
            pltpu.VMEM((LEVELS - 1, 2 * H, 384), BF16),
            pltpu.VMEM((2 * H, 640), BF16),
            pltpu.VMEM((2, 512 + 2 * PAD, 512), F32),
            pltpu.VMEM((2, 768 + 2 * PAD, TILE), F32),
            pltpu.VMEM((2, 768, TILE), BF16),
            pltpu.VMEM((2, 512, 512), BF16),
            pltpu.VMEM((LEVELS + 2, 8, 128), F32),
            pltpu.VMEM((ROWS, LEVELS + 2, 8, 128), F32),
            pltpu.SemaphoreType.DMA((DEPTH,)),
            pltpu.SemaphoreType.DMA((DEPTH,)),
            pltpu.SemaphoreType.DMA((len(HALO),)),
            pltpu.SemaphoreType.DMA((len(HALO),)),
            pltpu.SemaphoreType.DMA((len(PIECES), 32)),
            pltpu.SemaphoreType.DMA((len(PIECES), 32)),
            pltpu.SemaphoreType.DMA((ROWS,)),
            pltpu.SemaphoreType.DMA((ROWS,)),
        ],
        compiler_params=pltpu.CompilerParams(
            collective_id=0, has_side_effects=True, vmem_limit_bytes=67043328
        ),
    )(predicted_surpass_tally[0], observed_surpass_tally)
    return energy[None], skill[None]


def solution(mesh):
    return jax.shard_map(
        on_device,
        mesh=mesh,
        in_specs=(P("mem", "row", None), P("row", None)),
        out_specs=(P(None, None, "row", "mem"), P("mem", None, None)),
        check_vma=False,
    )
```
